128 devices in a mesh: section: 2 (over y_hi), fsdp: 8 (over z, core), replica: 8 (over x, y_lo).
Axes of the slice: x: 4, y: 4 (y_hi: 2, y_lo: 2; y = y_hi * 2 + y_lo), z: 4, core: 2. Of those that a mesh axis runs over, the one named last changes fastest.
Arguments:
- block_input: bfloat16 [8192, 1152], P(('fsdp', 'replica')), may hold values from -6 to 6
- out_cotangent: bfloat16 [8192, 1152], P(('fsdp', 'replica')), may hold values from -6 to 6
- seq_lengths: int32 [128], P(('fsdp', 'replica')), may hold values from 1 to 64, 5120 in all
- input_gain: bfloat16 [2, 1152], P('section', 'fsdp'), may hold values from 0.099609375 to 1.8984375
- query_weight: bfloat16 [2, 1152, 1024], P('section', 'fsdp'), may hold values from -0.1875 to 0.1875
- key_weight: bfloat16 [2, 1152, 256], P('section', 'fsdp'), may hold values from -0.1875 to 0.1875
- value_weight: bfloat16 [2, 1152, 256], P('section', 'fsdp'), may hold values from -0.1875 to 0.1875
- query_gain: bfloat16 [2, 256], P('section', 'fsdp'), may hold values from 0.099609375 to 1.8984375
- key_gain: bfloat16 [2, 256], P('section', 'fsdp'), may hold values from 0.099609375 to 1.8984375
- output_weight: bfloat16 [2, 1024, 1152], P('section', 'fsdp'), may hold values from -0.1875 to 0.1875
- attn_post_gain: bfloat16 [2, 1152], P('section', 'fsdp'), may hold values from 0.099609375 to 1.8984375
- ffw_pre_gain: bfloat16 [2, 1152], P('section', 'fsdp'), may hold values from 0.099609375 to 1.8984375
- gate_weight: bfloat16 [2, 1152, 6912], P('section', None, 'fsdp'), may hold values from -0.1875 to 0.1875
- up_weight: bfloat16 [2, 1152, 6912], P('section', None, 'fsdp'), may hold values from -0.1875 to 0.1875
- down_weight: bfloat16 [2, 6912, 1152], P('section', 'fsdp'), may hold values from -0.078125 to 0.078125
- ffw_post_gain: bfloat16 [2, 1152], P('section', 'fsdp'), may hold values from 0.099609375 to 1.8984375
Outputs:
- section_out: bfloat16 [2, 8192, 1152], P('section', ('fsdp', 'replica'))
- section_in_grad: bfloat16 [2, 8192, 1152], P('section', ('fsdp', 'replica'))
- input_gain_grad: float32 [2, 1152], P('section', 'fsdp')
- query_weight_grad: float32 [2, 1152, 1024], P('section', 'fsdp')
- key_weight_grad: float32 [2, 1152, 256], P('section', 'fsdp')
- value_weight_grad: float32 [2, 1152, 256], P('section', 'fsdp')
- query_gain_grad: float32 [2, 256], P('section', 'fsdp')
- key_gain_grad: float32 [2, 256], P('section', 'fsdp')
- output_weight_grad: float32 [2, 1024, 1152], P('section', 'fsdp')
- attn_post_gain_grad: float32 [2, 1152], P('section', 'fsdp')
- ffw_pre_gain_grad: float32 [2, 1152], P('section', 'fsdp')
- gate_weight_grad: float32 [2, 1152, 6912], P('section', None, 'fsdp')
- up_weight_grad: float32 [2, 1152, 6912], P('section', None, 'fsdp')
- down_weight_grad: float32 [2, 6912, 1152], P('section', 'fsdp')
- ffw_post_gain_grad: float32 [2, 1152], P('section', 'fsdp')
The draws below stay inside these ranges and needn't reach their ends.
Inputs may be any that keep to these rules, and one draw needn't show every extreme that they name: `seq_lengths`: some sequence has exactly 64 live tokens.
All inputs are finite; a program needn't handle non-finite values. No bound on the sum of `seq_lengths` on one device may be relied on, other than what follows from the above.
Results may differ from the reference program's by a relative error of at most 0.029.
Values may be sent and summed in bfloat16 or wider, within the bound.
A program may use at most 256 MiB of HBM per device.

```python
import math
import jax
import jax.numpy as jnp
import numpy as np
from jax import lax

D = 1152
FF = 6912
HEADS = 4
HEAD = 256
SEQ_ROWS = 64
SEQS = 128
TOKENS = 8192


def steps_of(key, dims, pieces, least, high):
    factor_of = 1.0
    for axis_at, blocks in pieces:
        draws = jax.random.uniform(jax.random.fold_in(jax.random.fold_in(key, 6), axis_at), (blocks,), jnp.float32, least / len(pieces), high / len(pieces))
        factor_of = factor_of * jnp.repeat(jnp.exp(draws), dims[axis_at] // blocks).reshape((-1,) + (1,) * (len(dims) - 1 - axis_at))
    return factor_of


def split_up(count, total, limit, lean):
    weights = [(1 << 20) // math.isqrt(standing ** lean) + 1 for standing in range(2, count + 1)]
    surplus, given = total - limit - (count - 1), [1] * (count - 1)
    while surplus > 0:
        free = [i for i in range(count - 1) if given[i] < limit]
        pool, remaining = sum([weights[i] for i in free]), surplus
        for i in free:
            more = min(limit - given[i], max(1, remaining * weights[i] // pool), surplus)
            given[i] = given[i] + more
            surplus = surplus - more
    return np.array([limit] + given)


def ragged(own_key, count, total, most, skew):
    if count == 2:
        one = jax.random.randint(own_key, (), max(1, total - most), min(most, total - 1) + 1)
        return jnp.stack([one, total - one])
    tallies = jnp.asarray(split_up(count, total, most, skew), jnp.int32)
    couples = (count - 1) // 2
    donor, receiver = tallies[1:1 + 2 * couples:2], tallies[2:2 + 2 * couples:2]
    room = jnp.minimum(donor - 1, most - receiver)
    passed = jax.random.randint(jax.random.fold_in(own_key, 1), (couples,), 0, 1 << 20) % (room + 1)
    tallies = tallies.at[1:1 + 2 * couples:2].set(donor - passed).at[2:2 + 2 * couples:2].set(receiver + passed)
    return tallies[jax.random.permutation(jax.random.fold_in(own_key, 2), count)]


def gaussian(key, shape, scale, bound, split=(), kind=jnp.bfloat16):
    result = jax.random.normal(key, shape, jnp.float32) * scale
    if len(split) > 0:
        result = steps_of(key, shape, split, -0.22, 0.18) * result
    return jnp.clip(result, min=-bound, max=bound).astype(kind)


def setup_inputs(seed: int = 0) -> dict:
    key_list = jax.random.split(jax.random.key(seed), 17)
    block_input = gaussian(key_list[0], (TOKENS, D), 1.0, 6.0, ((0, 64),))
    out_cotangent = gaussian(key_list[1], (TOKENS, D), 1.0, 6.0, ((0, 64),))
    seq_lengths = ragged(key_list[2], SEQS, SEQS * SEQ_ROWS * 5 // 8, SEQ_ROWS, 2).astype(jnp.int32)
    input_gain = jnp.clip(1.0 + 0.18 * jax.random.normal(key_list[3], (2, D), jnp.float32), 0.099609375, 1.8984375).astype(jnp.bfloat16)
    query_weight = gaussian(key_list[4], (2, D, HEADS * HEAD), D ** -0.5, 0.1875, ((0, 2), (1, 8)))
    key_weight = gaussian(key_list[5], (2, D, HEAD), D ** -0.5, 0.1875, ((0, 2), (1, 8)))
    value_weight = gaussian(key_list[6], (2, D, HEAD), D ** -0.5, 0.1875, ((0, 2), (1, 8)))
    query_gain = jnp.clip(1.0 + 0.18 * jax.random.normal(key_list[7], (2, HEAD), jnp.float32), 0.099609375, 1.8984375).astype(jnp.bfloat16)
    key_gain = jnp.clip(1.0 + 0.18 * jax.random.normal(key_list[8], (2, HEAD), jnp.float32), 0.099609375, 1.8984375).astype(jnp.bfloat16)
    output_weight = gaussian(key_list[9], (2, HEADS * HEAD, D), (HEADS * HEAD) ** -0.5, 0.1875, ((0, 2), (1, 8)))
    attn_post_gain = jnp.clip(1.0 + 0.18 * jax.random.normal(key_list[10], (2, D), jnp.float32), 0.099609375, 1.8984375).astype(jnp.bfloat16)
    ffw_pre_gain = jnp.clip(1.0 + 0.18 * jax.random.normal(key_list[11], (2, D), jnp.float32), 0.099609375, 1.8984375).astype(jnp.bfloat16)
    gate_weight = gaussian(key_list[12], (2, D, FF), D ** -0.5, 0.1875, ((0, 2), (2, 8)))
    up_weight = gaussian(key_list[13], (2, D, FF), D ** -0.5, 0.1875, ((0, 2), (2, 8)))
    down_weight = gaussian(key_list[14], (2, FF, D), FF ** -0.5, 0.078125, ((0, 2), (1, 8)))
    ffw_post_gain = jnp.clip(1.0 + 0.18 * jax.random.normal(key_list[15], (2, D), jnp.float32), 0.099609375, 1.8984375).astype(jnp.bfloat16)
    return {"block_input": block_input, "out_cotangent": out_cotangent, "seq_lengths": seq_lengths, "input_gain": input_gain, "query_weight": query_weight, "key_weight": key_weight, "value_weight": value_weight, "query_gain": query_gain, "key_gain": key_gain, "output_weight": output_weight, "attn_post_gain": attn_post_gain, "ffw_pre_gain": ffw_pre_gain, "gate_weight": gate_weight, "up_weight": up_weight, "down_weight": down_weight, "ffw_post_gain": ffw_post_gain}


EPSILON = 1e-06
ROPE_BASE = 10000.0
GELU_CUBIC = 0.044715
GELU_SCALE = math.sqrt(2.0 / math.pi)

def norm_scale(values):
    return lax.rsqrt(lax.optimization_barrier(jnp.mean(values * values, axis=-1, keepdims=True)) + EPSILON)

def norm_back(values, gain_vector, grad_result):
    inverse_rms = norm_scale(values)
    scaled = grad_result * gain_vector
    grad_values = inverse_rms * scaled - values * inverse_rms ** 3 * lax.optimization_barrier(jnp.mean(scaled * values, axis=-1, keepdims=True))
    gain_term = grad_result * values * inverse_rms
    return (grad_values, lax.optimization_barrier(jnp.sum(gain_term.reshape(-1, gain_term.shape[-1]), axis=0)))

def gelu_tanh(inputs):
    inner_arg = GELU_SCALE * (inputs + GELU_CUBIC * inputs ** 3)
    return 0.5 * inputs * (1.0 + jnp.tanh(inner_arg))

def gelu_slope(inputs):
    inner_arg = GELU_SCALE * (inputs + GELU_CUBIC * inputs ** 3)
    tangent = jnp.tanh(inner_arg)
    return 0.5 * (1.0 + tangent) + 0.5 * inputs * (1.0 - tangent * tangent) * GELU_SCALE * (1.0 + 3.0 * GELU_CUBIC * inputs * inputs)

def rope_tables(row_count, head_width):
    half_width = head_width // 2
    frequency = ROPE_BASE ** (-2.0 * jnp.arange(half_width, dtype=jnp.float32) / head_width)
    angles = jnp.arange(row_count, dtype=jnp.float32)[:, None] * frequency[None, :]
    return (jnp.cos(angles), jnp.sin(angles))

def rotate_pairs(vectors, cosine, sine_part):
    half_width = vectors.shape[-1] // 2
    first_half = vectors[..., :half_width]
    second_half = vectors[..., half_width:]
    return jnp.concatenate([first_half * cosine - second_half * sine_part, second_half * cosine + first_half * sine_part], axis=-1)

def attend_mask(lengths, row_count):
    position = jnp.arange(row_count, dtype=jnp.int32)
    causal = position[None, :] <= position[:, None]
    live_keys = position[None, :] < lengths[:, None]
    return causal[None, :, :] & live_keys[:, None, :]

def attend_scores(query_rot, key_rot):
    return jnp.einsum('sihd,sjd->shij', query_rot.astype(jnp.float32), key_rot.astype(jnp.float32)) * HEAD ** (-0.5)

def layer_forward(block_in, lengths, params):
    input_gain, query_weight, key_weight, value_weight, query_gain, key_gain, output_weight, attn_post_gain, ffw_pre_gain, gate_weight, up_weight, down_weight, ffw_post_gain = params
    seq_count, row_count, model_width = block_in.shape
    flat_rows = seq_count * row_count
    flat_in = block_in.reshape(flat_rows, model_width).astype(jnp.float32)
    normed_in = (flat_in * norm_scale(flat_in) * input_gain.astype(jnp.float32)).astype(jnp.bfloat16)
    query_raw = jnp.dot(normed_in, query_weight, preferred_element_type=jnp.float32).reshape(seq_count, row_count, HEADS, HEAD)
    key_raw = jnp.dot(normed_in, key_weight, preferred_element_type=jnp.float32).reshape(seq_count, row_count, HEAD)
    value_rows = jnp.dot(normed_in, value_weight, preferred_element_type=jnp.float32).astype(jnp.bfloat16).reshape(seq_count, row_count, HEAD)
    cosine, sine_part = rope_tables(row_count, HEAD)
    query_rot = rotate_pairs(query_raw * norm_scale(query_raw) * query_gain.astype(jnp.float32), cosine[:, None, :], sine_part[:, None, :]).astype(jnp.bfloat16)
    key_rot = rotate_pairs(key_raw * norm_scale(key_raw) * key_gain.astype(jnp.float32), cosine, sine_part).astype(jnp.bfloat16)
    allowed = attend_mask(lengths, row_count)[:, None, :, :]
    scores = attend_scores(query_rot, key_rot)
    exponent = jnp.where(allowed, jnp.exp(scores), 0.0)
    log_total = jnp.log(lax.optimization_barrier(jnp.sum(exponent, axis=-1)))
    probs = jnp.where(allowed, jnp.exp(scores - log_total[..., None]), 0.0)
    probs_b = probs.astype(jnp.bfloat16)
    context = jnp.einsum('shij,sjd->sihd', probs_b.astype(jnp.float32), value_rows.astype(jnp.float32))
    context_b = context.astype(jnp.bfloat16)
    attn_proj = jnp.dot(context_b.reshape(flat_rows, HEADS * HEAD), output_weight, preferred_element_type=jnp.float32)
    hidden = flat_in + attn_proj * norm_scale(attn_proj) * attn_post_gain.astype(jnp.float32)
    normed_mid = (hidden * norm_scale(hidden) * ffw_pre_gain.astype(jnp.float32)).astype(jnp.bfloat16)
    gate_rows = jnp.dot(normed_mid, gate_weight, preferred_element_type=jnp.float32)
    up_rows = jnp.dot(normed_mid, up_weight, preferred_element_type=jnp.float32)
    mixed = (gelu_tanh(gate_rows) * up_rows).astype(jnp.bfloat16)
    ffw_proj = jnp.dot(mixed, down_weight, preferred_element_type=jnp.float32)
    block_out = (hidden + ffw_proj * norm_scale(ffw_proj) * ffw_post_gain.astype(jnp.float32)).astype(jnp.bfloat16)
    saved = (flat_in, normed_in, query_raw, key_raw, query_rot, key_rot, value_rows, log_total, context, context_b, attn_proj, hidden, normed_mid, gate_rows, up_rows, mixed, ffw_proj)
    return (block_out.reshape(seq_count, row_count, model_width), saved)

def layer_backward(grad_result, lengths, params, saved):
    input_gain, query_weight, key_weight, value_weight, query_gain, key_gain, output_weight, attn_post_gain, ffw_pre_gain, gate_weight, up_weight, down_weight, ffw_post_gain = params
    flat_in, normed_in, query_raw, key_raw, query_rot, key_rot, value_rows, log_total, context, context_b, attn_proj, hidden, normed_mid, gate_rows, up_rows, mixed, ffw_proj = saved
    seq_count, row_count = (query_raw.shape[0], query_raw.shape[1])
    flat_rows = seq_count * row_count
    grad_ffw, sum_ffw_post = norm_back(ffw_proj, ffw_post_gain.astype(jnp.float32), grad_result)
    grad_ffw_b = grad_ffw.astype(jnp.bfloat16)
    grad_mixed = jnp.dot(grad_ffw_b, down_weight.T, preferred_element_type=jnp.float32)
    grad_gate_b = (grad_mixed * up_rows * gelu_slope(gate_rows)).astype(jnp.bfloat16)
    grad_up_b = (grad_mixed * gelu_tanh(gate_rows)).astype(jnp.bfloat16)
    grad_mid = jnp.dot(grad_gate_b, gate_weight.T, preferred_element_type=jnp.float32) + jnp.dot(grad_up_b, up_weight.T, preferred_element_type=jnp.float32)
    grad_hidden_part, sum_ffw_pre = norm_back(hidden, ffw_pre_gain.astype(jnp.float32), grad_mid)
    grad_hidden = grad_result + grad_hidden_part
    grad_attn, sum_attn_post = norm_back(attn_proj, attn_post_gain.astype(jnp.float32), grad_hidden)
    grad_attn_b = grad_attn.astype(jnp.bfloat16)
    grad_context_b = jnp.dot(grad_attn_b, output_weight.T, preferred_element_type=jnp.float32).astype(jnp.bfloat16).reshape(seq_count, row_count, HEADS, HEAD)
    allowed = attend_mask(lengths, row_count)[:, None, :, :]
    scores = attend_scores(query_rot, key_rot)
    probs = jnp.where(allowed, jnp.exp(scores - log_total[..., None]), 0.0)
    probs_b = probs.astype(jnp.bfloat16)
    grad_value = jnp.einsum('shij,sihd->sjd', probs_b.astype(jnp.float32), grad_context_b.astype(jnp.float32))
    grad_probs = jnp.einsum('sihd,sjd->shij', grad_context_b.astype(jnp.float32), value_rows.astype(jnp.float32))
    row_delta = jnp.transpose(lax.optimization_barrier(jnp.sum(grad_context_b.astype(jnp.float32) * context, axis=-1)), (0, 2, 1))
    grad_scores = (probs * (grad_probs - row_delta[..., None]) * HEAD ** (-0.5)).astype(jnp.bfloat16)
    grad_query_rot = jnp.einsum('shij,sjd->sihd', grad_scores.astype(jnp.float32), key_rot.astype(jnp.float32))
    grad_key_rot = jnp.einsum('shij,sihd->sjd', grad_scores.astype(jnp.float32), query_rot.astype(jnp.float32))
    cosine, sine_part = rope_tables(row_count, HEAD)
    grad_query_norm = rotate_pairs(grad_query_rot, cosine[:, None, :], -sine_part[:, None, :])
    grad_key_norm = rotate_pairs(grad_key_rot, cosine, -sine_part)
    grad_query, sum_query = norm_back(query_raw, query_gain.astype(jnp.float32), grad_query_norm)
    grad_key, sum_key = norm_back(key_raw, key_gain.astype(jnp.float32), grad_key_norm)
    grad_query_b = grad_query.astype(jnp.bfloat16).reshape(flat_rows, HEADS * HEAD)
    grad_key_b = grad_key.astype(jnp.bfloat16).reshape(flat_rows, HEAD)
    grad_value_b = grad_value.astype(jnp.bfloat16).reshape(flat_rows, HEAD)
    grad_normed = jnp.dot(grad_query_b, query_weight.T, preferred_element_type=jnp.float32) + jnp.dot(grad_key_b, key_weight.T, preferred_element_type=jnp.float32) + jnp.dot(grad_value_b, value_weight.T, preferred_element_type=jnp.float32)
    grad_in_part, sum_input = norm_back(flat_in, input_gain.astype(jnp.float32), grad_normed)
    grad_in = grad_hidden + grad_in_part
    parts = (sum_input, normed_in, grad_query_b, grad_key_b, grad_value_b, sum_query, sum_key, context_b.reshape(flat_rows, HEADS * HEAD), grad_attn_b, sum_attn_post, sum_ffw_pre, normed_mid, grad_gate_b, grad_up_b, mixed, grad_ffw_b, sum_ffw_post)
    return (grad_in, parts)

def outer_sum(left_rows, right_rows):
    return lax.dot_general(left_rows, right_rows, (((0,), (0,)), ((), ())), preferred_element_type=jnp.float32)

def weight_grads(parts):
    sum_input, normed_in, grad_query_b, grad_key_b, grad_value_b, sum_query, sum_key, context_rows, grad_attn_b, sum_attn_post, sum_ffw_pre, normed_mid, grad_gate_b, grad_up_b, mixed, grad_ffw_b, sum_ffw_post = parts
    return (sum_input, outer_sum(normed_in, grad_query_b), outer_sum(normed_in, grad_key_b), outer_sum(normed_in, grad_value_b), sum_query, sum_key, outer_sum(context_rows, grad_attn_b), sum_attn_post, sum_ffw_pre, outer_sum(normed_mid, grad_gate_b), outer_sum(normed_mid, grad_up_b), outer_sum(mixed, grad_ffw_b), sum_ffw_post)

def reference(block_input, out_cotangent, seq_lengths, input_gain, query_weight, key_weight, value_weight, query_gain, key_gain, output_weight, attn_post_gain, ffw_pre_gain, gate_weight, up_weight, down_weight, ffw_post_gain):
    stacked = (input_gain, query_weight, key_weight, value_weight, query_gain, key_gain, output_weight, attn_post_gain, ffw_pre_gain, gate_weight, up_weight, down_weight, ffw_post_gain)
    first_params = tuple((stacked_param[0] for stacked_param in stacked))
    second_params = tuple((stacked_param[1] for stacked_param in stacked))
    first_out, first_saved = layer_forward(block_input.reshape(SEQS, SEQ_ROWS, D), seq_lengths, first_params)
    second_out, second_saved = layer_forward(first_out, seq_lengths, second_params)
    position = jnp.arange(SEQ_ROWS, dtype=jnp.int32)
    live_rows = (position[None, :] < seq_lengths[:, None]).astype(jnp.float32).reshape(SEQS * SEQ_ROWS, 1)
    grad_top = out_cotangent.astype(jnp.float32) * live_rows
    second_grad, second_parts = layer_backward(grad_top, seq_lengths, second_params, second_saved)
    second_grad_b = second_grad.astype(jnp.bfloat16)
    first_grad, first_parts = layer_backward(second_grad_b.astype(jnp.float32), seq_lengths, first_params, first_saved)
    first_grad_b = first_grad.astype(jnp.bfloat16)
    section_out = jnp.stack([first_out.reshape(TOKENS, D), second_out.reshape(TOKENS, D)])
    section_in_grad = jnp.stack([first_grad_b, second_grad_b])
    first_terms = weight_grads(first_parts)
    second_terms = weight_grads(second_parts)
    grads = tuple((jnp.stack([left_term, right_term]) for left_term, right_term in zip(first_terms, second_terms)))
    return (section_out, section_in_grad, grads[0], grads[1], grads[2], grads[3], grads[4], grads[5], grads[6], grads[7], grads[8], grads[9], grads[10], grads[11], grads[12])
```

```python
import math

import jax
import jax.numpy as jnp
from jax import lax
from jax.sharding import PartitionSpec as P

D = 1152
HEADS = 4
HEAD = 256
MICRO = 2
SEQ_ROWS = 64


EPSILON = 1e-06
ROPE_BASE = 10000.0
GELU_CUBIC = 0.044715
GELU_SCALE = math.sqrt(2.0 / math.pi)


def shifted(shard, axis, by):
    devices = lax.axis_size(axis)
    pairs = [(i, i + by) for i in range(devices) if 0 <= i + by < devices]
    return lax.ppermute(shard, axis, pairs)


def norm_scale(values):
    return lax.rsqrt(jnp.mean(values * values, axis=-1, keepdims=True) + EPSILON)


def norm_back(values, gain_vector, grad_result):
    inverse_rms = norm_scale(values)
    scaled = grad_result * gain_vector
    grad_values = inverse_rms * scaled - values * inverse_rms**3 * jnp.mean(
        scaled * values, axis=-1, keepdims=True
    )
    gain_term = grad_result * values * inverse_rms
    return (grad_values, jnp.sum(gain_term.reshape(-1, gain_term.shape[-1]), axis=0))


def gelu_tanh(inputs):
    inner_arg = GELU_SCALE * (inputs + GELU_CUBIC * inputs**3)
    return 0.5 * inputs * (1.0 + jnp.tanh(inner_arg))


def gelu_slope(inputs):
    inner_arg = GELU_SCALE * (inputs + GELU_CUBIC * inputs**3)
    tangent = jnp.tanh(inner_arg)
    return 0.5 * (1.0 + tangent) + 0.5 * inputs * (1.0 - tangent * tangent) * GELU_SCALE * (
        1.0 + 3.0 * GELU_CUBIC * inputs * inputs
    )


def rope_tables(row_count, head_width):
    half_width = head_width // 2
    frequency = ROPE_BASE ** (-2.0 * jnp.arange(half_width, dtype=jnp.float32) / head_width)
    angles = jnp.arange(row_count, dtype=jnp.float32)[:, None] * frequency[None, :]
    return (jnp.cos(angles), jnp.sin(angles))


def rotate_pairs(vectors, cosine, sine_part):
    half_width = vectors.shape[-1] // 2
    first_half = vectors[..., :half_width]
    second_half = vectors[..., half_width:]
    return jnp.concatenate(
        [
            first_half * cosine - second_half * sine_part,
            second_half * cosine + first_half * sine_part,
        ],
        axis=-1,
    )


def attend_mask(lengths, row_count):
    position = jnp.arange(row_count, dtype=jnp.int32)
    causal = position[None, :] <= position[:, None]
    live_keys = position[None, :] < lengths[:, None]
    return causal[None, :, :] & live_keys[:, None, :]


def attend_scores(query_rot, key_rot):
    return jnp.einsum(
        "sihd,sjd->shij", query_rot.astype(jnp.float32), key_rot.astype(jnp.float32)
    ) * HEAD ** (-0.5)


def layer_forward(block_in, lengths, params):
    (
        input_gain,
        query_weight,
        key_weight,
        value_weight,
        query_gain,
        key_gain,
        output_weight,
        attn_post_gain,
        ffw_pre_gain,
        gate_weight,
        up_weight,
        down_weight,
        ffw_post_gain,
    ) = params
    seq_count, row_count, model_width = block_in.shape
    flat_rows = seq_count * row_count
    flat_in = block_in.reshape(flat_rows, model_width).astype(jnp.float32)
    normed_in = (flat_in * norm_scale(flat_in) * input_gain.astype(jnp.float32)).astype(
        jnp.bfloat16
    )
    query_raw = jnp.dot(normed_in, query_weight, preferred_element_type=jnp.float32).reshape(
        seq_count, row_count, HEADS, HEAD
    )
    key_raw = jnp.dot(normed_in, key_weight, preferred_element_type=jnp.float32).reshape(
        seq_count, row_count, HEAD
    )
    value_rows = (
        jnp.dot(normed_in, value_weight, preferred_element_type=jnp.float32)
        .astype(jnp.bfloat16)
        .reshape(seq_count, row_count, HEAD)
    )
    cosine, sine_part = rope_tables(row_count, HEAD)
    query_rot = rotate_pairs(
        query_raw * norm_scale(query_raw) * query_gain.astype(jnp.float32),
        cosine[:, None, :],
        sine_part[:, None, :],
    ).astype(jnp.bfloat16)
    key_rot = rotate_pairs(
        key_raw * norm_scale(key_raw) * key_gain.astype(jnp.float32), cosine, sine_part
    ).astype(jnp.bfloat16)
    allowed = attend_mask(lengths, row_count)[:, None, :, :]
    scores = attend_scores(query_rot, key_rot)
    exponent = jnp.where(allowed, jnp.exp(scores), 0.0)
    log_total = jnp.log(jnp.sum(exponent, axis=-1))
    probs = jnp.where(allowed, jnp.exp(scores - log_total[..., None]), 0.0)
    probs_b = probs.astype(jnp.bfloat16)
    context = jnp.einsum(
        "shij,sjd->sihd", probs_b.astype(jnp.float32), value_rows.astype(jnp.float32)
    )
    context_b = context.astype(jnp.bfloat16)
    attn_proj = jnp.dot(
        context_b.reshape(flat_rows, HEADS * HEAD),
        output_weight,
        preferred_element_type=jnp.float32,
    )
    hidden = flat_in + attn_proj * norm_scale(attn_proj) * attn_post_gain.astype(jnp.float32)
    normed_mid = (hidden * norm_scale(hidden) * ffw_pre_gain.astype(jnp.float32)).astype(
        jnp.bfloat16
    )
    gate_rows = jnp.dot(normed_mid, gate_weight, preferred_element_type=jnp.float32)
    up_rows = jnp.dot(normed_mid, up_weight, preferred_element_type=jnp.float32)
    mixed = (gelu_tanh(gate_rows) * up_rows).astype(jnp.bfloat16)
    ffw_proj = jnp.dot(mixed, down_weight, preferred_element_type=jnp.float32)
    block_out = (
        hidden + ffw_proj * norm_scale(ffw_proj) * ffw_post_gain.astype(jnp.float32)
    ).astype(jnp.bfloat16)
    saved = (
        flat_in,
        normed_in,
        query_raw,
        key_raw,
        query_rot,
        key_rot,
        value_rows,
        log_total,
        context,
        context_b,
        attn_proj,
        hidden,
        normed_mid,
        gate_rows,
        up_rows,
        mixed,
        ffw_proj,
    )
    return (block_out.reshape(seq_count, row_count, model_width), saved)


def layer_backward(grad_result, lengths, params, saved):
    (
        input_gain,
        query_weight,
        key_weight,
        value_weight,
        query_gain,
        key_gain,
        output_weight,
        attn_post_gain,
        ffw_pre_gain,
        gate_weight,
        up_weight,
        down_weight,
        ffw_post_gain,
    ) = params
    (
        flat_in,
        normed_in,
        query_raw,
        key_raw,
        query_rot,
        key_rot,
        value_rows,
        log_total,
        context,
        context_b,
        attn_proj,
        hidden,
        normed_mid,
        gate_rows,
        up_rows,
        mixed,
        ffw_proj,
    ) = saved
    seq_count, row_count = (query_raw.shape[0], query_raw.shape[1])
    flat_rows = seq_count * row_count
    grad_ffw, sum_ffw_post = norm_back(ffw_proj, ffw_post_gain.astype(jnp.float32), grad_result)
    grad_ffw_b = grad_ffw.astype(jnp.bfloat16)
    grad_mixed = jnp.dot(grad_ffw_b, down_weight.T, preferred_element_type=jnp.float32)
    grad_gate_b = (grad_mixed * up_rows * gelu_slope(gate_rows)).astype(jnp.bfloat16)
    grad_up_b = (grad_mixed * gelu_tanh(gate_rows)).astype(jnp.bfloat16)
    grad_mid = jnp.dot(grad_gate_b, gate_weight.T, preferred_element_type=jnp.float32) + jnp.dot(
        grad_up_b, up_weight.T, preferred_element_type=jnp.float32
    )
    grad_hidden_part, sum_ffw_pre = norm_back(hidden, ffw_pre_gain.astype(jnp.float32), grad_mid)
    grad_hidden = grad_result + grad_hidden_part
    grad_attn, sum_attn_post = norm_back(attn_proj, attn_post_gain.astype(jnp.float32), grad_hidden)
    grad_attn_b = grad_attn.astype(jnp.bfloat16)
    grad_context_b = (
        jnp.dot(grad_attn_b, output_weight.T, preferred_element_type=jnp.float32)
        .astype(jnp.bfloat16)
        .reshape(seq_count, row_count, HEADS, HEAD)
    )
    allowed = attend_mask(lengths, row_count)[:, None, :, :]
    scores = attend_scores(query_rot, key_rot)
    probs = jnp.where(allowed, jnp.exp(scores - log_total[..., None]), 0.0)
    probs_b = probs.astype(jnp.bfloat16)
    grad_value = jnp.einsum(
        "shij,sihd->sjd", probs_b.astype(jnp.float32), grad_context_b.astype(jnp.float32)
    )
    grad_probs = jnp.einsum(
        "sihd,sjd->shij", grad_context_b.astype(jnp.float32), value_rows.astype(jnp.float32)
    )
    row_delta = jnp.transpose(
        jnp.sum(grad_context_b.astype(jnp.float32) * context, axis=-1), (0, 2, 1)
    )
    grad_scores = (probs * (grad_probs - row_delta[..., None]) * HEAD ** (-0.5)).astype(
        jnp.bfloat16
    )
    grad_query_rot = jnp.einsum(
        "shij,sjd->sihd", grad_scores.astype(jnp.float32), key_rot.astype(jnp.float32)
    )
    grad_key_rot = jnp.einsum(
        "shij,sihd->sjd", grad_scores.astype(jnp.float32), query_rot.astype(jnp.float32)
    )
    cosine, sine_part = rope_tables(row_count, HEAD)
    grad_query_norm = rotate_pairs(grad_query_rot, cosine[:, None, :], -sine_part[:, None, :])
    grad_key_norm = rotate_pairs(grad_key_rot, cosine, -sine_part)
    grad_query, sum_query = norm_back(query_raw, query_gain.astype(jnp.float32), grad_query_norm)
    grad_key, sum_key = norm_back(key_raw, key_gain.astype(jnp.float32), grad_key_norm)
    grad_query_b = grad_query.astype(jnp.bfloat16).reshape(flat_rows, HEADS * HEAD)
    grad_key_b = grad_key.astype(jnp.bfloat16).reshape(flat_rows, HEAD)
    grad_value_b = grad_value.astype(jnp.bfloat16).reshape(flat_rows, HEAD)
    grad_normed = (
        jnp.dot(grad_query_b, query_weight.T, preferred_element_type=jnp.float32)
        + jnp.dot(grad_key_b, key_weight.T, preferred_element_type=jnp.float32)
        + jnp.dot(grad_value_b, value_weight.T, preferred_element_type=jnp.float32)
    )
    grad_in_part, sum_input = norm_back(flat_in, input_gain.astype(jnp.float32), grad_normed)
    grad_in = grad_hidden + grad_in_part
    parts = (
        sum_input,
        normed_in,
        grad_query_b,
        grad_key_b,
        grad_value_b,
        sum_query,
        sum_key,
        context_b.reshape(flat_rows, HEADS * HEAD),
        grad_attn_b,
        sum_attn_post,
        sum_ffw_pre,
        normed_mid,
        grad_gate_b,
        grad_up_b,
        mixed,
        grad_ffw_b,
        sum_ffw_post,
    )
    return (grad_in, parts)


def outer_sum(left_rows, right_rows):
    return lax.dot_general(
        left_rows, right_rows, (((0,), (0,)), ((), ())), preferred_element_type=jnp.float32
    )


def shards(
    block_input,
    out_cotangent,
    seq_lengths,
    input_gain,
    query_weight,
    key_weight,
    value_weight,
    query_gain,
    key_gain,
    output_weight,
    attn_post_gain,
    ffw_pre_gain,
    gate_weight,
    up_weight,
    down_weight,
    ffw_post_gain,
):
    section_index = lax.axis_index("section")
    gathered = (
        lax.all_gather(input_gain, "fsdp", axis=1, tiled=True),
        lax.all_gather(query_weight, "fsdp", axis=1, tiled=True),
        lax.all_gather(key_weight, "fsdp", axis=1, tiled=True),
        lax.all_gather(value_weight, "fsdp", axis=1, tiled=True),
        lax.all_gather(query_gain, "fsdp", axis=1, tiled=True),
        lax.all_gather(key_gain, "fsdp", axis=1, tiled=True),
        lax.all_gather(output_weight, "fsdp", axis=1, tiled=True),
        lax.all_gather(attn_post_gain, "fsdp", axis=1, tiled=True),
        lax.all_gather(ffw_pre_gain, "fsdp", axis=1, tiled=True),
        lax.all_gather(gate_weight, "fsdp", axis=2, tiled=True),
        lax.all_gather(up_weight, "fsdp", axis=2, tiled=True),
        lax.all_gather(down_weight, "fsdp", axis=1, tiled=True),
        lax.all_gather(ffw_post_gain, "fsdp", axis=1, tiled=True),
    )
    params = tuple((full_param[0] for full_param in gathered))
    micro_inputs = block_input.reshape(MICRO, SEQ_ROWS, D)
    micro_cotangents = out_cotangent.reshape(MICRO, SEQ_ROWS, D)
    received = jnp.zeros((1, SEQ_ROWS, D), jnp.bfloat16)
    forward_outs = []
    forward_saved = []
    for tick_index in range(MICRO + 1):
        own_rows = micro_inputs[min(tick_index, MICRO - 1)][None]
        current = jnp.where(section_index == 0, own_rows, received)
        micro_index = jnp.clip(tick_index - section_index, 0, MICRO - 1)
        lengths = lax.dynamic_slice_in_dim(seq_lengths, micro_index, 1)
        block_out, saved = layer_forward(current, lengths, params)
        forward_outs.append(block_out)
        forward_saved.append(saved)
        if tick_index < MICRO:
            received = shifted(block_out, "section", 1)
    section_out = lax.dynamic_slice_in_dim(
        jnp.stack(forward_outs), section_index, MICRO, 0
    ).reshape(1, MICRO * SEQ_ROWS, D)
    position = jnp.arange(SEQ_ROWS, dtype=jnp.int32)
    received_grad = jnp.zeros((SEQ_ROWS, D), jnp.bfloat16)
    grads_sent = []
    parts_list = []
    for tick_index in range(MICRO + 1):
        late_micro = max(MICRO - 1 - tick_index, 0)
        early_micro = min(MICRO - tick_index, MICRO - 1)
        micro_index = jnp.where(section_index == 1, late_micro, early_micro).astype(jnp.int32)
        lengths = lax.dynamic_slice_in_dim(seq_lengths, micro_index, 1)
        live_rows = (position < lengths[0]).astype(jnp.float32)[:, None]
        top_grad = micro_cotangents[late_micro].astype(jnp.float32) * live_rows
        grad_result = jnp.where(section_index == 1, top_grad, received_grad.astype(jnp.float32))
        grad_in, parts = layer_backward(
            grad_result, lengths, params, forward_saved[MICRO - tick_index]
        )
        grad_in_b = grad_in.astype(jnp.bfloat16)
        grads_sent.append(grad_in_b)
        parts_list.append(parts)
        if tick_index < MICRO:
            received_grad = shifted(grad_in_b, "section", -1)
    first_useful = 1 - section_index
    useful_grads = lax.dynamic_slice_in_dim(jnp.stack(grads_sent), first_useful, MICRO, 0)
    section_in_grad = jnp.flip(useful_grads, axis=0).reshape(1, MICRO * SEQ_ROWS, D)
    selected = []
    for part_index in range(len(parts_list[0])):
        stacked_part = jnp.stack([tick_parts[part_index] for tick_parts in parts_list])
        useful_part = lax.dynamic_slice_in_dim(stacked_part, first_useful, MICRO, 0)
        if useful_part.ndim == 2:
            selected.append(jnp.sum(useful_part, axis=0))
        else:
            selected.append(useful_part.reshape(MICRO * useful_part.shape[1], useful_part.shape[2]))
    (
        sum_input,
        normed_rows,
        grad_query_b,
        grad_key_b,
        grad_value_b,
        sum_query,
        sum_key,
        context_rows,
        grad_attn_b,
        sum_attn_post,
        sum_ffw_pre,
        normed_mid,
        grad_gate_b,
        grad_up_b,
        mixed,
        grad_ffw_b,
        sum_ffw_post,
    ) = tuple(selected)
    gain_shards = (
        lax.psum_scatter(sum_input, "fsdp", scatter_dimension=0, tiled=True),
        lax.psum_scatter(sum_query, "fsdp", scatter_dimension=0, tiled=True),
        lax.psum_scatter(sum_key, "fsdp", scatter_dimension=0, tiled=True),
        lax.psum_scatter(sum_attn_post, "fsdp", scatter_dimension=0, tiled=True),
        lax.psum_scatter(sum_ffw_pre, "fsdp", scatter_dimension=0, tiled=True),
        lax.psum_scatter(sum_ffw_post, "fsdp", scatter_dimension=0, tiled=True),
    )
    gathered_rows = (
        lax.all_to_all(normed_rows, "fsdp", split_axis=1, concat_axis=0, tiled=True),
        lax.all_to_all(context_rows, "fsdp", split_axis=1, concat_axis=0, tiled=True),
        lax.all_to_all(mixed, "fsdp", split_axis=1, concat_axis=0, tiled=True),
        lax.all_to_all(grad_gate_b, "fsdp", split_axis=1, concat_axis=0, tiled=True),
        lax.all_to_all(grad_up_b, "fsdp", split_axis=1, concat_axis=0, tiled=True),
        lax.all_gather(grad_query_b, "fsdp", axis=0, tiled=True),
        lax.all_gather(grad_key_b, "fsdp", axis=0, tiled=True),
        lax.all_gather(grad_value_b, "fsdp", axis=0, tiled=True),
        lax.all_gather(grad_attn_b, "fsdp", axis=0, tiled=True),
        lax.all_gather(normed_mid, "fsdp", axis=0, tiled=True),
        lax.all_gather(grad_ffw_b, "fsdp", axis=0, tiled=True),
    )
    own_parts = gathered_rows[:5]
    full_parts = gathered_rows[5:]
    normed_own, context_own, mixed_own, gate_own, up_own = own_parts
    query_all, key_all, value_all, attn_all, normed_mid_all, ffw_all = full_parts
    query_shard = outer_sum(normed_own, query_all)
    key_shard = outer_sum(normed_own, key_all)
    value_shard = outer_sum(normed_own, value_all)
    output_shard = outer_sum(context_own, attn_all)
    gate_shard = outer_sum(normed_mid_all, gate_own)
    up_shard = outer_sum(normed_mid_all, up_own)
    down_shard = outer_sum(mixed_own, ffw_all)
    totals = (
        lax.psum(gain_shards[0].astype(jnp.bfloat16), "replica").astype(jnp.float32),
        lax.psum(query_shard.astype(jnp.bfloat16), "replica").astype(jnp.float32),
        lax.psum(key_shard.astype(jnp.bfloat16), "replica").astype(jnp.float32),
        lax.psum(value_shard.astype(jnp.bfloat16), "replica").astype(jnp.float32),
        lax.psum(gain_shards[1].astype(jnp.bfloat16), "replica").astype(jnp.float32),
        lax.psum(gain_shards[2].astype(jnp.bfloat16), "replica").astype(jnp.float32),
        lax.psum(output_shard.astype(jnp.bfloat16), "replica").astype(jnp.float32),
        lax.psum(gain_shards[3].astype(jnp.bfloat16), "replica").astype(jnp.float32),
        lax.psum(gain_shards[4].astype(jnp.bfloat16), "replica").astype(jnp.float32),
        lax.psum(gate_shard.astype(jnp.bfloat16), "replica").astype(jnp.float32),
        lax.psum(up_shard.astype(jnp.bfloat16), "replica").astype(jnp.float32),
        lax.psum(down_shard.astype(jnp.bfloat16), "replica").astype(jnp.float32),
        lax.psum(gain_shards[5].astype(jnp.bfloat16), "replica").astype(jnp.float32),
    )
    return (
        section_out,
        section_in_grad,
        totals[0][None],
        totals[1][None],
        totals[2][None],
        totals[3][None],
        totals[4][None],
        totals[5][None],
        totals[6][None],
        totals[7][None],
        totals[8][None],
        totals[9][None],
        totals[10][None],
        totals[11][None],
        totals[12][None],
    )


def solution(mesh):
    placed = (
        P(("fsdp", "replica"), None),
        P(("fsdp", "replica"), None),
        P(("fsdp", "replica")),
        P("section", "fsdp"),
        P("section", "fsdp", None),
        P("section", "fsdp", None),
        P("section", "fsdp", None),
        P("section", "fsdp"),
        P("section", "fsdp"),
        P("section", "fsdp", None),
        P("section", "fsdp"),
        P("section", "fsdp"),
        P("section", None, "fsdp"),
        P("section", None, "fsdp"),
        P("section", "fsdp", None),
        P("section", "fsdp"),
    )
    return jax.shard_map(
        shards,
        mesh=mesh,
        in_specs=placed,
        out_specs=(
            P("section", ("fsdp", "replica"), None),
            P("section", ("fsdp", "replica"), None),
            P("section", "fsdp"),
            P("section", "fsdp", None),
            P("section", "fsdp", None),
            P("section", "fsdp", None),
            P("section", "fsdp"),
            P("section", "fsdp"),
            P("section", "fsdp", None),
            P("section", "fsdp"),
            P("section", "fsdp"),
            P("section", None, "fsdp"),
            P("section", None, "fsdp"),
            P("section", "fsdp", None),
            P("section", "fsdp"),
        ),
        check_vma=False,
    )
```
